32 devices in a mesh: aux: 8 (over y, x, core), orb: 4 (over z).
Axes of the slice: x: 2, y: 2, z: 4, core: 2. Of those that a mesh axis runs over, the one named last changes fastest.
Arguments:
- tiles: float32 [256, 64, 4096], P(('aux', 'orb')), may hold values from -6 to 6
- tile_list: int32 [4, 256], P(None, ('aux', 'orb')), may hold values from 0 to 255, as said below
- orb_factor: float32 [4096, 256], P('orb'), may hold values from -30 to 30
- nu_factor: float32 [512, 256], replicated, may hold values from -30 to 30
Outputs:
- aux_factor: float32 [16384, 256], P('aux')
- orb_updated: float32 [4096, 256], P('orb')
- nu_updated: float32 [512, 256], replicated
The draws below stay inside these ranges and needn't reach their ends.
Inputs may be any that keep to these rules, and one draw needn't show every extreme that they name: `tile_list`: slot s belongs to the device s // 8 along aux+orb; for that device with aux index a and orb index o, row 0 lies in [a * 32, (a + 1) * 32), row 1 in [o * 16, (o + 1) * 16), row 2 below 8. The coordinates of one device's slots are distinct. Row 3 is 0 or 1: 1 on a device's first slots and 0 on the rest; every device has at least one flagged slot and some device has all 8 flagged.
All inputs are finite; a program needn't handle non-finite values.
Results may differ from the reference program's by a relative error of at most 0.0003.
Values sent between devices are 32-bit elements; how exact they have to be, the bound alone decides.
A program may use at most 256 MiB of HBM per device.

```python
import jax
import jax.numpy as jnp
from jax import lax

P_SIZE = 16384
MU = 4096
NU = 512
R = 256
TILE = 64
TILES_DEV = 8
NTILES = 256
BLOCK_P = 32
BLOCK_M = 16


def factor_draw(key, row_count):
    key_list = jax.random.split(key, 4)
    noise_part = jnp.clip(jax.random.normal(key_list[0], (row_count, R), jnp.float32), -4.0, 4.0)
    shared = jnp.clip(jax.random.normal(key_list[1], (row_count, 12), jnp.float32), -4.0, 4.0)
    amplitudes = jax.random.uniform(key_list[2], (12, 1), jnp.float32, 0.3, 1.5)
    mixing = jax.random.normal(key_list[3], (12, R), jnp.float32) * amplitudes
    values = noise_part + jnp.dot(shared, mixing, preferred_element_type=jnp.float32)
    return jnp.clip(values, -30.0, 30.0)


def draw_orb_factor(key, part):
    return factor_draw(jax.random.fold_in(key, 11), MU)


def draw_nu_factor(key, part):
    return factor_draw(jax.random.fold_in(key, 13), NU)


def draw_tile_list(key, part):
    devices_all = NTILES // TILES_DEV
    orb_span = MU // TILE // BLOCK_M
    nu_tiles = NU // TILE
    region = BLOCK_P * BLOCK_M * nu_tiles
    key_list = jax.random.split(jax.random.fold_in(key, 7), 4)

    def pick_cells(device_key):
        return jax.random.permutation(device_key, region)[:TILES_DEV]
    cell_ids = jax.vmap(pick_cells)(jax.random.split(key_list[0], devices_all)).astype(jnp.int32)
    device_ids = jnp.arange(devices_all, dtype=jnp.int32)[:, None]
    shifted = (cell_ids + (region - 1 - cell_ids[:, :1])) % region
    is_last = device_ids == devices_all - 1
    cell_ids = jnp.where(is_last, shifted, cell_ids).astype(jnp.int32)
    first_tile = device_ids // orb_span * BLOCK_P + cell_ids // (BLOCK_M * nu_tiles)
    second_tile = device_ids % orb_span * BLOCK_M + cell_ids // nu_tiles % BLOCK_M
    third_tile = cell_ids % nu_tiles
    top_count = max(1, TILES_DEV // 2)
    counts = jax.random.randint(key_list[1], (devices_all, 1), 1, top_count + 1)
    picked_full = jax.random.randint(key_list[2], (devices_all, 1), 0, 8) == 0
    chosen = jax.random.randint(key_list[3], (), 0, devices_all)
    filled = picked_full | (device_ids == chosen)
    counts = jnp.where(filled, TILES_DEV, counts)
    slot_ids = jnp.arange(TILES_DEV, dtype=jnp.int32)[None, :]
    live_flags = (slot_ids < counts).astype(jnp.int32)
    stacked = jnp.stack([first_tile, second_tile, third_tile, live_flags])
    return stacked.reshape(4, NTILES).astype(jnp.int32)


def levels(stream_key, dims, pieces, least, top_value):
    gain, own = 1.0, jax.random.fold_in(stream_key, 6)
    for position, parts in pieces:
        draws = jnp.exp(jax.random.uniform(jax.random.fold_in(own, position), (parts,), jnp.float32, least / len(pieces), top_value / len(pieces)))
        gain = gain * jnp.repeat(draws, dims[position] // parts).reshape([-1 if axis == position else 1 for axis in range(len(dims))])
    return gain


def gaussian(key, dims, spread, limit, cuts=(), kind=jnp.bfloat16):
    factor_of = levels(key, dims, cuts, -0.22, 0.18) if cuts else 1.0
    result = jax.random.normal(key, dims, jnp.float32) * spread * factor_of
    return jnp.minimum(jnp.maximum(result, -limit), limit).astype(kind)


def setup_inputs(seed: int = 0) -> dict:
    key_of = jax.random.split(jax.random.key(seed), 5)
    tiles = gaussian(key_of[0], (NTILES, TILE, TILE * TILE), 1.0, 6.0, ((0, 32),), jnp.float32)
    tile_list = draw_tile_list(jax.random.fold_in(key_of[4], 71), 0)
    orb_factor = draw_orb_factor(jax.random.fold_in(key_of[4], 71), 0)
    nu_factor = draw_nu_factor(jax.random.fold_in(key_of[4], 71), 0)
    return {"tiles": tiles, "tile_list": tile_list, "orb_factor": orb_factor, "nu_factor": nu_factor}


ridge_weight = 0.5
epsilon = 1e-06
highest = lax.Precision.HIGHEST

def gram_of(matrix):
    return jnp.dot(matrix.T.astype(jnp.float32), matrix.astype(jnp.float32), precision=highest, preferred_element_type=jnp.float32)

def solve_rows(system, targets):
    factor_lower = jnp.linalg.cholesky(system)
    return jax.scipy.linalg.cho_solve((factor_lower, True), targets.T).T

def add_rows(running, addition, start):
    previous = lax.dynamic_slice_in_dim(running, start, addition.shape[0], 0)
    return lax.dynamic_update_slice_in_dim(running, previous + addition, start, 0)

def mode_first(tiles, tile_list, orb_factor, nu_factor):

    def tile_step(running, tile_item):
        tile_block, coords = tile_item
        nu_block = lax.dynamic_slice_in_dim(nu_factor, (coords[2] * TILE).astype(jnp.int32), TILE, 0)
        orb_block = lax.dynamic_slice_in_dim(orb_factor, (coords[1] * TILE).astype(jnp.int32), TILE, 0)
        contracted = jnp.dot(tile_block.reshape(TILE * TILE, TILE).astype(jnp.float32), nu_block.astype(jnp.float32), precision=highest, preferred_element_type=jnp.float32).reshape(TILE, TILE, R)
        addition = lax.optimization_barrier(jnp.sum(contracted * orb_block[None], axis=1)) * coords[3].astype(jnp.float32)
        return (add_rows(running, addition, (coords[0] * TILE).astype(jnp.int32)), None)
    running, _ = lax.scan(tile_step, jnp.zeros((P_SIZE, R), jnp.float32), (tiles, tile_list.T))
    return running

def mode_second(tiles, tile_list, aux_factor, nu_factor):

    def tile_step(running, tile_item):
        tile_block, coords = tile_item
        nu_block = lax.dynamic_slice_in_dim(nu_factor, (coords[2] * TILE).astype(jnp.int32), TILE, 0)
        aux_block = lax.dynamic_slice_in_dim(aux_factor, (coords[0] * TILE).astype(jnp.int32), TILE, 0)
        contracted = jnp.dot(tile_block.reshape(TILE * TILE, TILE).astype(jnp.float32), nu_block.astype(jnp.float32), precision=highest, preferred_element_type=jnp.float32).reshape(TILE, TILE, R)
        addition = lax.optimization_barrier(jnp.sum(contracted * aux_block[:, None, :], axis=0)) * coords[3].astype(jnp.float32)
        return (add_rows(running, addition, (coords[1] * TILE).astype(jnp.int32)), None)
    running, _ = lax.scan(tile_step, jnp.zeros((MU, R), jnp.float32), (tiles, tile_list.T))
    return running

def mode_third(tiles, tile_list, aux_factor, orb_factor):

    def tile_step(running, tile_item):
        tile_block, coords = tile_item
        aux_block = lax.dynamic_slice_in_dim(aux_factor, (coords[0] * TILE).astype(jnp.int32), TILE, 0)
        orb_block = lax.dynamic_slice_in_dim(orb_factor, (coords[1] * TILE).astype(jnp.int32), TILE, 0)
        contracted = lax.dot_general(tile_block.astype(jnp.float32), aux_block.astype(jnp.float32), (((0,), (0,)), ((), ())), precision=highest, preferred_element_type=jnp.float32).reshape(TILE, TILE, R)
        addition = lax.optimization_barrier(jnp.sum(contracted * orb_block[:, None, :], axis=0)) * coords[3].astype(jnp.float32)
        return (add_rows(running, addition, (coords[2] * TILE).astype(jnp.int32)), None)
    running, _ = lax.scan(tile_step, jnp.zeros((NU, R), jnp.float32), (tiles, tile_list.T))
    return running

def normalize(values, row_count):
    scales = jnp.sqrt(lax.optimization_barrier(jnp.sum(values * values, axis=0)) / row_count + epsilon)
    scaled = values / scales
    return (scaled, gram_of(scaled) / row_count)

def reference(tiles, tile_list, orb_factor, nu_factor):
    identity = jnp.eye(R, dtype=jnp.float32)
    s_orb = gram_of(orb_factor) / MU
    s_nu = gram_of(nu_factor) / NU
    first_terms = mode_first(tiles, tile_list, orb_factor, nu_factor)
    a_new = solve_rows(s_orb * s_nu + ridge_weight * identity, first_terms)
    aux_factor, s_first = normalize(a_new, P_SIZE)
    second_terms = mode_second(tiles, tile_list, aux_factor, nu_factor)
    b_new = solve_rows(s_first * s_nu + ridge_weight * identity, second_terms)
    orb_updated, s_second = normalize(b_new, MU)
    third_terms = mode_third(tiles, tile_list, aux_factor, orb_updated)
    c_new = solve_rows(s_first * s_second + ridge_weight * identity, third_terms)
    nu_updated, _ = normalize(c_new, NU)
    return (aux_factor, orb_updated, nu_updated)
```

```python
import functools

import jax
import jax.numpy as jnp
from jax import lax
from jax.experimental import pallas as pl
from jax.experimental.pallas import tpu as pltpu
from jax.sharding import PartitionSpec as P

P_SIZE = 16384
MU = 4096
NU = 512

ridge_weight = 0.5
epsilon = 1e-06
highest = lax.Precision.HIGHEST
f32 = jnp.float32
bf16 = jnp.bfloat16
PANEL = 32


def gram_of(matrix):
    return jnp.dot(matrix.T, matrix, precision=highest, preferred_element_type=f32)


def split_two(x):
    high = x.astype(bf16)
    return high, (x - high.astype(f32)).astype(bf16)


def split_three(x):
    high = x.astype(bf16)
    rest = x - high.astype(f32)
    middle = rest.astype(bf16)
    return high, middle, (rest - middle.astype(f32)).astype(bf16)


def first_kernel(edge, index_ref, x_ref, orb_ref, nu_ref, out_ref):
    slot = pl.program_id(0)
    second_at = pl.multiple_of(index_ref[1, slot] * edge, edge)
    third_at = pl.multiple_of(index_ref[2, slot] * edge, edge)
    nu_block = nu_ref[pl.ds(third_at, edge), :]
    orb_block = orb_ref[pl.ds(second_at, edge), :]
    rank = nu_block.shape[1]
    group = 4
    total = jnp.zeros((edge, rank), f32)
    for start in range(0, edge, group):
        x_high, x_low = split_two(x_ref[0, :, start * edge:(start + group) * edge])
        stacked = jnp.concatenate([x_high, x_low], axis=0)
        product = jnp.concatenate(
            [nu_block * orb_block[j:j + 1, :] for j in range(start, start + group)], axis=0
        )
        high, low = split_two(product)
        main = jnp.dot(stacked, high, preferred_element_type=f32)
        rest = jnp.dot(x_high, low, preferred_element_type=f32)
        total += main[:edge] + (main[edge:] + rest)
    out_ref[...] = jnp.where(index_ref[3, slot] > 0, total, 0.0)


def solve_kernel(edge, blocks, at_ref, part_ref, inverse_ref, a_ref, gram_ref, total_ref):
    total_ref[...] = jnp.zeros_like(total_ref)

    def add_block(block, carry):
        rows = pl.ds(pl.multiple_of(at_ref[block] * edge, edge), edge)
        total_ref[rows, :] += part_ref[pl.ds(pl.multiple_of(block * edge, edge), edge), :]
        return carry

    lax.fori_loop(0, blocks, add_block, 0)
    inverse = inverse_ref[...]
    chunk = min(256, total_ref.shape[0])
    gram_ref[...] = jnp.zeros_like(gram_ref)

    def apply(step, carry):
        rows = pl.ds(pl.multiple_of(step * chunk, chunk), chunk)
        solved = jnp.dot(total_ref[rows, :], inverse, precision=highest, preferred_element_type=f32)
        a_ref[rows, :] = solved
        gram_ref[...] += lax.dot_general(
            solved, solved, (((0,), (0,)), ((), ())), precision=highest, preferred_element_type=f32
        )
        return carry

    lax.fori_loop(0, total_ref.shape[0] // chunk, apply, 0)


def second_kernel(edge, index_ref, x_ref, a_ref, nu_ref, e_ref, out_ref):
    slot = pl.program_id(0)
    first_at = pl.multiple_of(index_ref[0, slot] * edge, edge)
    second_at = pl.multiple_of(index_ref[1, slot] * edge, edge)
    third_at = pl.multiple_of(index_ref[2, slot] * edge, edge)
    live = index_ref[3, slot] > 0

    @pl.when(slot == 0)
    def _():
        out_ref[...] = jnp.zeros_like(out_ref)

    nu_block = nu_ref[pl.ds(third_at, edge), :]
    a_high, a_low = split_two(a_ref[pl.ds(first_at, edge), :])
    weights = jnp.concatenate([a_high, a_high, a_low, a_low], axis=0)
    group = 8
    for start in range(0, edge, group):
        x_high, x_low = split_two(x_ref[0, :, start * edge:(start + group) * edge])
        turned = jnp.concatenate([x_high, x_low], axis=0).T
        e = jnp.dot(
            jnp.concatenate([turned, turned], axis=1), weights, preferred_element_type=f32
        )
        e_ref[0, start * edge:(start + group) * edge, :] = e
        sums = jnp.sum(e.reshape(group, edge, e.shape[1]) * nu_block[None], axis=1)
        rows = pl.ds(pl.multiple_of(second_at + start, group), group)
        out_ref[rows, :] += jnp.where(live, sums, 0.0)


def third_kernel(edge, index_ref, e_ref, b_ref, out_ref):
    slot = pl.program_id(0)
    second_at = pl.multiple_of(index_ref[1, slot] * edge, edge)
    third_at = pl.multiple_of(index_ref[2, slot] * edge, edge)

    @pl.when(slot == 0)
    def _():
        out_ref[...] = jnp.zeros_like(out_ref)

    b_block = b_ref[pl.ds(second_at, edge), :]
    total = jnp.zeros((edge, b_block.shape[1]), f32)
    for j in range(edge):
        total += e_ref[0, j * edge:(j + 1) * edge, :] * b_block[j:j + 1, :]
    out_ref[pl.ds(third_at, edge), :] += jnp.where(index_ref[3, slot] > 0, total, 0.0)


def eye_mask(n):
    return lax.broadcasted_iota(jnp.int32, (n, n), 0) == lax.broadcasted_iota(jnp.int32, (n, n), 1)


def unit_gram(gram, rows):
    diagonal = jnp.where(eye_mask(gram.shape[0]), gram, 0.0)
    along = jnp.sqrt(jnp.sum(diagonal, axis=0, keepdims=True) / rows + epsilon)
    down = jnp.sqrt(jnp.sum(diagonal, axis=1, keepdims=True) / rows + epsilon)
    return gram / down / along / rows, along


def sweep_inverse(a_ref):
    n = a_ref.shape[0]
    lane = lax.broadcasted_iota(jnp.int32, (PANEL, n), 1)
    row = lax.broadcasted_iota(jnp.int32, (PANEL, n), 0)

    def panel_step(step, carry):
        before = a_ref[:PANEL, :]
        panel = before
        for k in range(0, PANEL, 2):
            first = jnp.broadcast_to(panel[:, k:k + 1], panel.shape)
            second = jnp.broadcast_to(panel[:, k + 1:k + 2], panel.shape)
            at_first, at_second = lane == k, lane == k + 1
            unit_first = jnp.where(at_second[:1], 0.0, panel[k:k + 1, :])
            unit_first = jnp.where(at_first[:1], 1.0, unit_first)
            unit_second = jnp.where(at_first[:1], 0.0, panel[k + 1:k + 2, :])
            unit_second = jnp.where(at_second[:1], 1.0, unit_second)
            inverse = 1.0 / first[k:k + 1, :]
            across = second[k:k + 1, :]
            factor = first[k + 1:k + 2, :] * inverse
            inverse_schur = 1.0 / (second[k + 1:k + 2, :] - factor * across)
            new_second = (unit_second - factor * unit_first) * inverse_schur
            new_first = (unit_first - across * new_second) * inverse
            kept = jnp.where(at_first | at_second, 0.0, panel)
            panel = kept - first * new_first - second * new_second
            panel = jnp.where(row == k, new_first, jnp.where(row == k + 1, new_second, panel))
        own = lane < PANEL
        update = jnp.where(own, -panel, panel)
        w_high, w_middle, w_low = split_three(before)
        z_high, z_middle, z_low = split_three(update)
        left = jnp.concatenate([w_low, w_middle, w_high, w_middle, w_high, w_high], axis=0)
        right = jnp.concatenate([z_high, z_middle, z_low, z_high, z_middle, z_high], axis=0)
        change = lax.dot_general(
            left, right, (((0,), (0,)), ((), ())), preferred_element_type=f32
        )
        others = jnp.where(own[:1], 0.0, a_ref[PANEL:, :]) - change[PANEL:, :]
        a_ref[:n - PANEL, :] = pltpu.roll(others, n - PANEL, 1)
        a_ref[n - PANEL:, :] = pltpu.roll(update, n - PANEL, 1)
        return carry

    lax.fori_loop(0, n // PANEL, panel_step, 0)


def inverse_kernel(left_rows, right_rows, left_ref, right_ref, inverse_ref, scale_ref, a_ref):
    left = left_ref[...]
    if left_rows:
        left, scale_ref[...] = unit_gram(left, left_rows)
    else:
        scale_ref[...] = jnp.ones_like(scale_ref)
    right = right_ref[...]
    if right_rows:
        right, _ = unit_gram(right, right_rows)
    n = left.shape[0]
    a_ref[...] = left * right + jnp.where(eye_mask(n), ridge_weight, 0.0)
    sweep_inverse(a_ref)
    inverse_ref[...] = -a_ref[...]


def inverse_of(left, right, left_rows, right_rows, name):
    n = left.shape[0]
    whole = pl.BlockSpec(memory_space=pltpu.VMEM)
    return pl.pallas_call(
        functools.partial(inverse_kernel, left_rows, right_rows),
        out_shape=(jax.ShapeDtypeStruct((n, n), f32), jax.ShapeDtypeStruct((1, n), f32)),
        in_specs=[whole, whole],
        out_specs=(whole, whole),
        scratch_shapes=[pltpu.VMEM((n, n), f32)],
        compiler_params=pltpu.CompilerParams(vmem_limit_bytes=16 << 20),
        cost_estimate=pl.CostEstimate(flops=10**9, bytes_accessed=4 * n * n * 4, transcendentals=0),
        name=name,
    )(left, right)


def per_device(tiles, tile_list, orb_factor, nu_factor):
    slots, edge = tiles.shape[0], tiles.shape[1]
    rank = nu_factor.shape[1]
    first_rows = P_SIZE // lax.axis_size("aux")
    orb_rows = orb_factor.shape[0]
    orb_size = lax.axis_size("orb")
    tile_width = tiles.shape[2]
    index = tile_list - jnp.stack(
        [
            lax.axis_index("aux") * (first_rows // edge),
            lax.axis_index("orb") * (orb_rows // edge),
            jnp.int32(0),
            jnp.int32(0),
        ]
    ).astype(jnp.int32)[:, None]
    tile_spec = pl.BlockSpec((1, edge, tile_width), lambda s, i: (s, 0, 0))

    def full(rows):
        return pl.BlockSpec((rows, rank), lambda s, i: (0, 0))

    own_row = lax.broadcasted_iota(jnp.int32, (orb_size, slots), 0) == lax.axis_index("orb")
    own_at = jnp.where(own_row, index[0].astype(f32)[None], 0.0)
    s_nu = gram_of(nu_factor) / NU
    gram_orb, slot_at = lax.psum((gram_of(orb_factor), own_at), "orb")
    s_orb = gram_orb / MU
    slot_at = slot_at.astype(jnp.int32).reshape(-1)

    parts = pl.pallas_call(
        functools.partial(first_kernel, edge),
        out_shape=jax.ShapeDtypeStruct((slots * edge, rank), f32),
        grid_spec=pltpu.PrefetchScalarGridSpec(
            num_scalar_prefetch=1,
            grid=(slots,),
            in_specs=[tile_spec, full(orb_rows), full(nu_factor.shape[0])],
            out_specs=pl.BlockSpec((edge, rank), lambda s, i: (s, 0)),
        ),
        name="mode_first",
    )(index, tiles, orb_factor, nu_factor)
    gathered = lax.all_gather(parts, "orb", axis=0, tiled=True)
    inverse_first, _ = inverse_of(s_orb, s_nu, 0, 0, "inverse_first")
    blocks = slots * orb_size
    vmem = pl.BlockSpec(memory_space=pltpu.VMEM)
    a_new, gram_a = pl.pallas_call(
        functools.partial(solve_kernel, edge, blocks),
        out_shape=(
            jax.ShapeDtypeStruct((first_rows, rank), f32),
            jax.ShapeDtypeStruct((rank, rank), f32),
        ),
        in_specs=[pl.BlockSpec(memory_space=pltpu.SMEM), vmem, vmem],
        out_specs=(vmem, vmem),
        scratch_shapes=[pltpu.VMEM((first_rows, rank), f32)],
        name="solve_first",
    )(slot_at, gathered, inverse_first)
    gram_a = lax.psum(gram_a, "aux")

    e_all, partial_second = pl.pallas_call(
        functools.partial(second_kernel, edge),
        out_shape=(
            jax.ShapeDtypeStruct((slots, tile_width, rank), f32),
            jax.ShapeDtypeStruct((orb_rows, rank), f32),
        ),
        grid_spec=pltpu.PrefetchScalarGridSpec(
            num_scalar_prefetch=1,
            grid=(slots,),
            in_specs=[tile_spec, full(first_rows), full(nu_factor.shape[0])],
            out_specs=(
                pl.BlockSpec((1, tile_width, rank), lambda s, i: (s, 0, 0)),
                full(orb_rows),
            ),
        ),
        name="mode_second",
    )(index, tiles, a_new, nu_factor)
    sums_first = jnp.sum(jnp.where(eye_mask(rank), gram_a, 0.0), axis=0)
    scale_first = jnp.sqrt(sums_first / P_SIZE + epsilon)
    second_sums = lax.psum(partial_second / scale_first, "aux")
    inverse_second, _ = inverse_of(gram_a, s_nu, P_SIZE, 0, "inverse_second")
    aux_factor = a_new / scale_first
    b_new = jnp.dot(second_sums, inverse_second, precision=highest, preferred_element_type=f32)
    gram_b = lax.psum(gram_of(b_new), "orb")

    partial_third = pl.pallas_call(
        functools.partial(third_kernel, edge),
        out_shape=jax.ShapeDtypeStruct((nu_factor.shape[0], rank), f32),
        grid_spec=pltpu.PrefetchScalarGridSpec(
            num_scalar_prefetch=1,
            grid=(slots,),
            in_specs=[
                pl.BlockSpec((1, tile_width, rank), lambda s, i: (s, 0, 0)),
                full(orb_rows),
            ],
            out_specs=full(nu_factor.shape[0]),
        ),
        name="mode_third",
    )(index, e_all, b_new)
    third_sums = lax.psum(partial_third, ("aux", "orb"))
    inverse_third, scale_second = inverse_of(gram_b, gram_a, MU, P_SIZE, "inverse_third")
    orb_updated = b_new / scale_second
    c_new = jnp.dot(
        third_sums / scale_first / scale_second,
        inverse_third,
        precision=highest,
        preferred_element_type=f32,
    )
    scale_third = jnp.sqrt(jnp.sum(c_new * c_new, axis=0) / NU + epsilon)
    nu_updated = c_new / scale_third
    return (aux_factor, orb_updated, nu_updated)


def solution(mesh):
    return jax.shard_map(
        per_device,
        mesh=mesh,
        in_specs=(P(("aux", "orb"), None, None), P(None, ("aux", "orb")), P("orb", None), P()),
        out_specs=(P("aux", None), P("orb", None), P()),
        check_vma=False,
    )
```

```python
import functools

import jax
import jax.numpy as jnp
from jax import lax
from jax.experimental import pallas as pl
from jax.experimental.pallas import tpu as pltpu
from jax.sharding import PartitionSpec as P

P_SIZE = 16384
MU = 4096
NU = 512

ridge_weight = 0.5
epsilon = 1e-06
highest = lax.Precision.HIGHEST
f32 = jnp.float32
bf16 = jnp.bfloat16
PANEL = 32


MESH = pl.DeviceIdType.MESH


def reduce_kernel(steps, x_ref, out_ref, sum_ref, all_ref, *scratch):
    count = len(steps)
    landing = scratch[:count]
    send_sem, recv_sem = scratch[count:]
    bits, partners = [], []
    for axis, bit in steps:
        here = lax.axis_index(axis)
        value = (here // (1 << bit)) % 2
        bits.append(value)
        partners.append({axis: here + (1 - 2 * value) * (1 << bit)})
    barrier = pltpu.get_barrier_semaphore()
    for partner in partners:
        pl.semaphore_signal(barrier, inc=1, device_id=partner, device_id_type=MESH)
    pl.semaphore_wait(barrier, count)
    sum_ref[...] = x_ref[...]
    length = sum_ref.shape[0]
    start = jnp.int32(0)
    kept = []
    for step in range(count):
        length //= 2
        mine = pl.multiple_of(start + bits[step] * length, 8)
        other = pl.multiple_of(start + (1 - bits[step]) * length, 8)
        copy = pltpu.make_async_remote_copy(
            src_ref=sum_ref.at[pl.ds(other, length), :],
            dst_ref=landing[step],
            send_sem=send_sem.at[step],
            recv_sem=recv_sem.at[step],
            device_id=partners[step],
            device_id_type=MESH,
        )
        copy.start()
        copy.wait()
        sum_ref[pl.ds(mine, length), :] += landing[step][...]
        start = mine
        kept.append((mine, length))
    mine, length = kept[-1]
    all_ref[pl.ds(mine, length), :] = sum_ref[pl.ds(mine, length), :]
    for step in reversed(range(count)):
        mine, length = kept[step]
        rows = all_ref.at[pl.ds(mine, length), :]
        copy = pltpu.make_async_remote_copy(
            src_ref=rows,
            dst_ref=rows,
            send_sem=send_sem.at[count + step],
            recv_sem=recv_sem.at[count + step],
            device_id=partners[step],
            device_id_type=MESH,
        )
        copy.start()
        copy.wait()
    out_ref[...] = all_ref[...]


def all_reduce(x, axes, number, name):
    steps = []
    for axis in axes:
        size = lax.axis_size(axis)
        if size & (size - 1):
            return lax.psum(x, axes)
        steps += [(axis, bit) for bit in range(size.bit_length() - 1)]
    rows, columns = x.shape
    if rows % (8 << len(steps)):
        return lax.psum(x, axes)
    count = len(steps)
    vmem = pl.BlockSpec(memory_space=pltpu.VMEM)
    return pl.pallas_call(
        functools.partial(reduce_kernel, tuple(steps)),
        out_shape=jax.ShapeDtypeStruct(x.shape, f32),
        in_specs=[vmem],
        out_specs=vmem,
        scratch_shapes=[pltpu.VMEM((rows, columns), f32)] * 2
        + [pltpu.VMEM((rows >> (step + 1), columns), f32) for step in range(count)]
        + [pltpu.SemaphoreType.DMA((2 * count,)), pltpu.SemaphoreType.DMA((2 * count,))],
        compiler_params=pltpu.CompilerParams(collective_id=number, has_side_effects=True),
        name=name,
    )(x)


def gram_of(matrix):
    return jnp.dot(matrix.T, matrix, precision=highest, preferred_element_type=f32)


def split_two(x):
    high = x.astype(bf16)
    return high, (x - high.astype(f32)).astype(bf16)


def split_three(x):
    high = x.astype(bf16)
    rest = x - high.astype(f32)
    middle = rest.astype(bf16)
    return high, middle, (rest - middle.astype(f32)).astype(bf16)


def first_kernel(edge, index_ref, x_ref, orb_ref, nu_ref, out_ref):
    slot = pl.program_id(0)
    second_at = pl.multiple_of(index_ref[1, slot] * edge, edge)
    third_at = pl.multiple_of(index_ref[2, slot] * edge, edge)
    nu_block = nu_ref[pl.ds(third_at, edge), :]
    orb_block = orb_ref[pl.ds(second_at, edge), :]
    rank = nu_block.shape[1]
    group = 4
    total = jnp.zeros((edge, rank), f32)
    for start in range(0, edge, group):
        x_high, x_low = split_two(x_ref[0, :, start * edge:(start + group) * edge])
        stacked = jnp.concatenate([x_high, x_low], axis=0)
        product = jnp.concatenate(
            [nu_block * orb_block[j:j + 1, :] for j in range(start, start + group)], axis=0
        )
        high, low = split_two(product)
        main = jnp.dot(stacked, high, preferred_element_type=f32)
        rest = jnp.dot(x_high, low, preferred_element_type=f32)
        total += main[:edge] + (main[edge:] + rest)
    out_ref[...] = jnp.where(index_ref[3, slot] > 0, total, 0.0)


def solve_kernel(edge, blocks, at_ref, part_ref, inverse_ref, a_ref, gram_ref, total_ref):
    total_ref[...] = jnp.zeros_like(total_ref)

    def add_block(block, carry):
        rows = pl.ds(pl.multiple_of(at_ref[block] * edge, edge), edge)
        total_ref[rows, :] += part_ref[pl.ds(pl.multiple_of(block * edge, edge), edge), :]
        return carry

    lax.fori_loop(0, blocks, add_block, 0)
    inverse = inverse_ref[...]
    chunk = min(256, total_ref.shape[0])
    gram_ref[...] = jnp.zeros_like(gram_ref)

    def apply(step, carry):
        rows = pl.ds(pl.multiple_of(step * chunk, chunk), chunk)
        solved = jnp.dot(total_ref[rows, :], inverse, precision=highest, preferred_element_type=f32)
        a_ref[rows, :] = solved
        gram_ref[...] += lax.dot_general(
            solved, solved, (((0,), (0,)), ((), ())), precision=highest, preferred_element_type=f32
        )
        return carry

    lax.fori_loop(0, total_ref.shape[0] // chunk, apply, 0)


def second_kernel(edge, index_ref, x_ref, a_ref, nu_ref, e_ref, out_ref):
    slot = pl.program_id(0)
    first_at = pl.multiple_of(index_ref[0, slot] * edge, edge)
    second_at = pl.multiple_of(index_ref[1, slot] * edge, edge)
    third_at = pl.multiple_of(index_ref[2, slot] * edge, edge)
    live = index_ref[3, slot] > 0

    @pl.when(slot == 0)
    def _():
        out_ref[...] = jnp.zeros_like(out_ref)

    nu_block = nu_ref[pl.ds(third_at, edge), :]
    a_high, a_low = split_two(a_ref[pl.ds(first_at, edge), :])
    weights = jnp.concatenate([a_high, a_high, a_low, a_low], axis=0)
    group = 8
    for start in range(0, edge, group):
        x_high, x_low = split_two(x_ref[0, :, start * edge:(start + group) * edge])
        turned = jnp.concatenate([x_high, x_low], axis=0).T
        e = jnp.dot(
            jnp.concatenate([turned, turned], axis=1), weights, preferred_element_type=f32
        )
        e_ref[0, start * edge:(start + group) * edge, :] = e
        sums = jnp.sum(e.reshape(group, edge, e.shape[1]) * nu_block[None], axis=1)
        rows = pl.ds(pl.multiple_of(second_at + start, group), group)
        out_ref[rows, :] += jnp.where(live, sums, 0.0)


def third_kernel(edge, index_ref, e_ref, b_ref, out_ref):
    slot = pl.program_id(0)
    second_at = pl.multiple_of(index_ref[1, slot] * edge, edge)
    third_at = pl.multiple_of(index_ref[2, slot] * edge, edge)

    @pl.when(slot == 0)
    def _():
        out_ref[...] = jnp.zeros_like(out_ref)

    b_block = b_ref[pl.ds(second_at, edge), :]
    total = jnp.zeros((edge, b_block.shape[1]), f32)
    for j in range(edge):
        total += e_ref[0, j * edge:(j + 1) * edge, :] * b_block[j:j + 1, :]
    out_ref[pl.ds(third_at, edge), :] += jnp.where(index_ref[3, slot] > 0, total, 0.0)


def eye_mask(n):
    return lax.broadcasted_iota(jnp.int32, (n, n), 0) == lax.broadcasted_iota(jnp.int32, (n, n), 1)


def unit_gram(gram, rows):
    diagonal = jnp.where(eye_mask(gram.shape[0]), gram, 0.0)
    along = jnp.sqrt(jnp.sum(diagonal, axis=0, keepdims=True) / rows + epsilon)
    down = jnp.sqrt(jnp.sum(diagonal, axis=1, keepdims=True) / rows + epsilon)
    return gram / down / along / rows, along


def sweep_inverse(a_ref):
    n = a_ref.shape[0]
    lane = lax.broadcasted_iota(jnp.int32, (PANEL, n), 1)
    row = lax.broadcasted_iota(jnp.int32, (PANEL, n), 0)

    def panel_step(step, carry):
        before = a_ref[:PANEL, :]
        panel = before
        for k in range(0, PANEL, 2):
            first = jnp.broadcast_to(panel[:, k:k + 1], panel.shape)
            second = jnp.broadcast_to(panel[:, k + 1:k + 2], panel.shape)
            at_first, at_second = lane == k, lane == k + 1
            unit_first = jnp.where(at_second[:1], 0.0, panel[k:k + 1, :])
            unit_first = jnp.where(at_first[:1], 1.0, unit_first)
            unit_second = jnp.where(at_first[:1], 0.0, panel[k + 1:k + 2, :])
            unit_second = jnp.where(at_second[:1], 1.0, unit_second)
            inverse = 1.0 / first[k:k + 1, :]
            across = second[k:k + 1, :]
            factor = first[k + 1:k + 2, :] * inverse
            inverse_schur = 1.0 / (second[k + 1:k + 2, :] - factor * across)
            new_second = (unit_second - factor * unit_first) * inverse_schur
            new_first = (unit_first - across * new_second) * inverse
            kept = jnp.where(at_first | at_second, 0.0, panel)
            panel = kept - first * new_first - second * new_second
            panel = jnp.where(row == k, new_first, jnp.where(row == k + 1, new_second, panel))
        own = lane < PANEL
        update = jnp.where(own, -panel, panel)
        w_high, w_middle, w_low = split_three(before)
        z_high, z_middle, z_low = split_three(update)
        left = jnp.concatenate([w_low, w_middle, w_high, w_middle, w_high, w_high], axis=0)
        right = jnp.concatenate([z_high, z_middle, z_low, z_high, z_middle, z_high], axis=0)
        change = lax.dot_general(
            left, right, (((0,), (0,)), ((), ())), preferred_element_type=f32
        )
        others = jnp.where(own[:1], 0.0, a_ref[PANEL:, :]) - change[PANEL:, :]
        a_ref[:n - PANEL, :] = pltpu.roll(others, n - PANEL, 1)
        a_ref[n - PANEL:, :] = pltpu.roll(update, n - PANEL, 1)
        return carry

    lax.fori_loop(0, n // PANEL, panel_step, 0)


def inverse_kernel(left_rows, right_rows, left_ref, right_ref, inverse_ref, scale_ref, a_ref):
    left = left_ref[...]
    if left_rows:
        left, scale_ref[...] = unit_gram(left, left_rows)
    else:
        scale_ref[...] = jnp.ones_like(scale_ref)
    right = right_ref[...]
    if right_rows:
        right, _ = unit_gram(right, right_rows)
    n = left.shape[0]
    a_ref[...] = left * right + jnp.where(eye_mask(n), ridge_weight, 0.0)
    sweep_inverse(a_ref)
    inverse_ref[...] = -a_ref[...]


def inverse_of(left, right, left_rows, right_rows, name):
    n = left.shape[0]
    whole = pl.BlockSpec(memory_space=pltpu.VMEM)
    return pl.pallas_call(
        functools.partial(inverse_kernel, left_rows, right_rows),
        out_shape=(jax.ShapeDtypeStruct((n, n), f32), jax.ShapeDtypeStruct((1, n), f32)),
        in_specs=[whole, whole],
        out_specs=(whole, whole),
        scratch_shapes=[pltpu.VMEM((n, n), f32)],
        compiler_params=pltpu.CompilerParams(vmem_limit_bytes=16 << 20),
        cost_estimate=pl.CostEstimate(flops=10**9, bytes_accessed=4 * n * n * 4, transcendentals=0),
        name=name,
    )(left, right)


def per_device(tiles, tile_list, orb_factor, nu_factor):
    slots, edge = tiles.shape[0], tiles.shape[1]
    rank = nu_factor.shape[1]
    first_rows = P_SIZE // lax.axis_size("aux")
    orb_rows = orb_factor.shape[0]
    orb_size = lax.axis_size("orb")
    tile_width = tiles.shape[2]
    index = tile_list - jnp.stack(
        [
            lax.axis_index("aux") * (first_rows // edge),
            lax.axis_index("orb") * (orb_rows // edge),
            jnp.int32(0),
            jnp.int32(0),
        ]
    ).astype(jnp.int32)[:, None]
    tile_spec = pl.BlockSpec((1, edge, tile_width), lambda s, i: (s, 0, 0))

    def full(rows):
        return pl.BlockSpec((rows, rank), lambda s, i: (0, 0))

    own_row = lax.broadcasted_iota(jnp.int32, (orb_size, slots), 0) == lax.axis_index("orb")
    own_at = jnp.where(own_row, index[0].astype(f32)[None], 0.0)
    s_nu = gram_of(nu_factor) / NU
    table = jnp.pad(own_at, ((0, -orb_size % 8), (0, rank - slots)))
    joined = lax.psum(jnp.concatenate([gram_of(orb_factor), table], axis=0), "orb")
    s_orb = joined[:rank] / MU
    slot_at = joined[rank:rank + orb_size, :slots].astype(jnp.int32).reshape(-1)

    parts = pl.pallas_call(
        functools.partial(first_kernel, edge),
        out_shape=jax.ShapeDtypeStruct((slots * edge, rank), f32),
        grid_spec=pltpu.PrefetchScalarGridSpec(
            num_scalar_prefetch=1,
            grid=(slots,),
            in_specs=[tile_spec, full(orb_rows), full(nu_factor.shape[0])],
            out_specs=pl.BlockSpec((edge, rank), lambda s, i: (s, 0)),
        ),
        name="mode_first",
    )(index, tiles, orb_factor, nu_factor)
    gathered = lax.all_gather(parts, "orb", axis=0, tiled=True)
    inverse_first, _ = inverse_of(s_orb, s_nu, 0, 0, "inverse_first")
    blocks = slots * orb_size
    vmem = pl.BlockSpec(memory_space=pltpu.VMEM)
    a_new, gram_a = pl.pallas_call(
        functools.partial(solve_kernel, edge, blocks),
        out_shape=(
            jax.ShapeDtypeStruct((first_rows, rank), f32),
            jax.ShapeDtypeStruct((rank, rank), f32),
        ),
        in_specs=[pl.BlockSpec(memory_space=pltpu.SMEM), vmem, vmem],
        out_specs=(vmem, vmem),
        scratch_shapes=[pltpu.VMEM((first_rows, rank), f32)],
        name="solve_first",
    )(slot_at, gathered, inverse_first)
    gram_a = all_reduce(gram_a, ("aux",), 1, "sum_gram_first")

    e_all, partial_second = pl.pallas_call(
        functools.partial(second_kernel, edge),
        out_shape=(
            jax.ShapeDtypeStruct((slots, tile_width, rank), f32),
            jax.ShapeDtypeStruct((orb_rows, rank), f32),
        ),
        grid_spec=pltpu.PrefetchScalarGridSpec(
            num_scalar_prefetch=1,
            grid=(slots,),
            in_specs=[tile_spec, full(first_rows), full(nu_factor.shape[0])],
            out_specs=(
                pl.BlockSpec((1, tile_width, rank), lambda s, i: (s, 0, 0)),
                full(orb_rows),
            ),
        ),
        name="mode_second",
    )(index, tiles, a_new, nu_factor)
    sums_first = jnp.sum(jnp.where(eye_mask(rank), gram_a, 0.0), axis=0)
    scale_first = jnp.sqrt(sums_first / P_SIZE + epsilon)
    second_sums = all_reduce(partial_second / scale_first, ("aux",), 2, "sum_second")
    inverse_second, _ = inverse_of(gram_a, s_nu, P_SIZE, 0, "inverse_second")
    aux_factor = a_new / scale_first
    b_new = jnp.dot(second_sums, inverse_second, precision=highest, preferred_element_type=f32)
    gram_b = all_reduce(gram_of(b_new), ("orb",), 3, "sum_gram_second")

    partial_third = pl.pallas_call(
        functools.partial(third_kernel, edge),
        out_shape=jax.ShapeDtypeStruct((nu_factor.shape[0], rank), f32),
        grid_spec=pltpu.PrefetchScalarGridSpec(
            num_scalar_prefetch=1,
            grid=(slots,),
            in_specs=[
                pl.BlockSpec((1, tile_width, rank), lambda s, i: (s, 0, 0)),
                full(orb_rows),
            ],
            out_specs=full(nu_factor.shape[0]),
        ),
        name="mode_third",
    )(index, e_all, b_new)
    third_sums = all_reduce(partial_third, ("aux", "orb"), 4, "sum_third")
    inverse_third, scale_second = inverse_of(gram_b, gram_a, MU, P_SIZE, "inverse_third")
    orb_updated = b_new / scale_second
    c_new = jnp.dot(
        third_sums / scale_first / scale_second,
        inverse_third,
        precision=highest,
        preferred_element_type=f32,
    )
    scale_third = jnp.sqrt(jnp.sum(c_new * c_new, axis=0) / NU + epsilon)
    nu_updated = c_new / scale_third
    return (aux_factor, orb_updated, nu_updated)


def solution(mesh):
    return jax.shard_map(
        per_device,
        mesh=mesh,
        in_specs=(P(("aux", "orb"), None, None), P(None, ("aux", "orb")), P("orb", None), P()),
        out_specs=(P("aux", None), P("orb", None), P()),
        check_vma=False,
    )
```
